32 devices in a mesh: dp: 4 (over z), row: 4 (over x, core), col: 2 (over y).
Axes of the slice: x: 2, y: 2, z: 4, core: 2. Of those that a mesh axis runs over, the one named last changes fastest.
Arguments:
- tokens: bfloat16 [16384, 1024], P(('dp', 'col'), 'row'), may hold values from -11 to 11
- segments: int32 [32, 512], P(('dp', 'row')), may hold values from 0 to 3, never falling along the last dimension, each value on 1 to 256 neighbouring positions
- cotangent: bfloat16 [16384, 1024], P(('dp', 'col'), 'row'), may hold values from -6 to 6
- in_proj: float32 [1024, 3, 1024], P('row', None, 'col'), may hold values from -0.1875 to 0.1875
- entry_bias: float32 [2, 1024], P(None, 'col'), may hold values from -0.3 to 0.3
- out_proj: float32 [1024, 1024], P('col', 'row'), may hold values from -2 to 2
- up_proj: float32 [1024, 4096], P('row', 'col'), may hold values from -0.1875 to 0.1875
- hidden_bias: float32 [4096], P('col'), may hold values from -3 to 3
- down_proj: float32 [4096, 1024], P('col', 'row'), may hold values from -0.09375 to 0.09375
- norm_gains: float32 [2, 1024], P(None, 'row'), may hold values from 0.5 to 1.5
- row_biases: float32 [4, 1024], P(None, 'row'), may hold values from -3 to 3
- moments_in: float32 [2, 1024, 3, 1024], P(None, 'row', None, 'col'), as said below
- moments_entry: float32 [2, 2, 1024], P(None, None, 'col'), as said below
- moments_out: float32 [2, 1024, 1024], P(None, 'col', 'row'), as said below
- moments_up: float32 [2, 1024, 4096], P(None, 'row', 'col'), as said below
- moments_hidden: float32 [2, 4096], P(None, 'col'), as said below
- moments_down: float32 [2, 4096, 1024], P(None, 'col', 'row'), as said below
- moments_gains: float32 [2, 2, 1024], P(None, None, 'row'), as said below
- moments_biases: float32 [2, 4, 1024], P(None, None, 'row'), as said below
Outputs:
- layer_out: bfloat16 [16384, 1024], P(('dp', 'col'), 'row')
- input_grad: bfloat16 [16384, 1024], P(('dp', 'col'), 'row')
- grad_in: float32 [1024, 3, 1024], P('row', None, 'col')
- grad_entry: float32 [2, 1024], P(None, 'col')
- grad_out: float32 [1024, 1024], P('col', 'row')
- grad_up: float32 [1024, 4096], P('row', 'col')
- grad_hidden: float32 [4096], P('col')
- grad_down: float32 [4096, 1024], P('col', 'row')
- grad_gains: float32 [2, 1024], P(None, 'row')
- grad_biases: float32 [4, 1024], P(None, 'row')
- update_in: float32 [1024, 3, 1024], P('row', None, 'col')
- update_entry: float32 [2, 1024], P(None, 'col')
- update_out: float32 [1024, 1024], P('col', 'row')
- update_up: float32 [1024, 4096], P('row', 'col')
- update_hidden: float32 [4096], P('col')
- update_down: float32 [4096, 1024], P('col', 'row')
- update_gains: float32 [2, 1024], P(None, 'row')
- update_biases: float32 [4, 1024], P(None, 'row')
- state_in: float32 [2, 1024, 3, 1024], P(None, 'row', None, 'col')
- state_entry: float32 [2, 2, 1024], P(None, None, 'col')
- state_out: float32 [2, 1024, 1024], P(None, 'col', 'row')
- state_up: float32 [2, 1024, 4096], P(None, 'row', 'col')
- state_hidden: float32 [2, 4096], P(None, 'col')
- state_down: float32 [2, 4096, 1024], P(None, 'col', 'row')
- state_gains: float32 [2, 2, 1024], P(None, None, 'row')
- state_biases: float32 [2, 4, 1024], P(None, None, 'row')
The draws below stay inside these ranges and needn't reach their ends.
Inputs may be any that keep to these rules, and one draw needn't show every extreme that they name: `segments`: each sequence holds at most 4 documents of 1 to 256 tokens, one of exactly 256; numbers never fall along a sequence. `moments_in`: index 0 holds first moments, index 1 positive second moments. `moments_entry`: index 0 holds first moments, index 1 positive second moments. `moments_out`: index 0 holds first moments, index 1 positive second moments. `moments_up`: index 0 holds first moments, index 1 positive second moments. `moments_hidden`: index 0 holds first moments, index 1 positive second moments. `moments_down`: index 0 holds first moments, index 1 positive second moments. `moments_gains`: index 0 holds first moments, index 1 positive second moments. `moments_biases`: index 0 holds first moments, index 1 positive second moments.
All inputs are finite; a program needn't handle non-finite values.
Results may differ from the reference program's by a relative error of at most 0.015.
The reference program's roundings to bfloat16 on the way count: a program that leaves them out, or rounds other values in their place, can miss the bound.
Values may be sent and summed in bfloat16 or wider, within the bound.
No kernel may reach another device: no remote copies, remote signals or barrier semaphores. Data moves between devices by JAX's collectives and lax.ppermute only.
A program may use at most 256 MiB of HBM per device.

```python
import math
import jax
import jax.numpy as jnp
import numpy as np
from jax import lax

D = 1024
FF = 4096
HD = 64
HEADS = 16
L = 512
SEGS = 4
MOST = 256
SEQ_GRP = 2
SEQS = 32
TOKENS = 16384


def draw_tokens(key, part):
    column = jnp.arange(D, dtype=jnp.float32) / D
    ramp = 0.6 + 1.2 * column
    return (jax.random.truncated_normal(jax.random.fold_in(key, 11), -6.0, 6.0, (TOKENS, D), jnp.float32) * ramp).astype(jnp.bfloat16)


def moment_pair(key, shape, grad_scale, salt):
    own_key = jax.random.fold_in(key, salt)
    first_mom = jax.random.normal(jax.random.fold_in(own_key, 21), shape, jnp.float32) * (0.06 * grad_scale)
    spread = jax.random.uniform(jax.random.fold_in(own_key, 22), shape, jnp.float32, -0.69, 0.69)
    second_mom = jnp.exp(spread) * (0.002 * grad_scale * grad_scale)
    return jnp.stack([first_mom, second_mom])


def draw_moments_in(key, part):
    return moment_pair(key, (D, 3, D), TOKENS ** 0.5, 31)


def draw_moments_entry(key, part):
    return moment_pair(key, (2, D), TOKENS ** 0.5, 32)


def draw_moments_out(key, part):
    return moment_pair(key, (D, D), ((SEGS / L) ** 0.5 + 0.05) * TOKENS ** 0.5, 33)


def draw_moments_up(key, part):
    return moment_pair(key, (D, FF), 0.3 * TOKENS ** 0.5, 34)


def draw_moments_hidden(key, part):
    return moment_pair(key, (FF,), 0.3 * TOKENS ** 0.5, 35)


def draw_moments_down(key, part):
    return moment_pair(key, (FF, D), 0.6 * TOKENS ** 0.5, 36)


def draw_moments_gains(key, part):
    return moment_pair(key, (2, D), TOKENS ** 0.5, 37)


def draw_moments_biases(key, part):
    return moment_pair(key, (4, D), TOKENS ** 0.5, 38)


def steps_of(rng, dims, shards, least, largest):
    def one(axis_at, blocks):
        steps = jax.random.uniform(jax.random.fold_in(jax.random.fold_in(rng, 6), axis_at), (blocks,), jnp.float32, least / len(shards), largest / len(shards))
        return jnp.repeat(jnp.exp(steps), dims[axis_at] // blocks).reshape((-1,) + (1,) * (len(dims) - axis_at - 1))

    level = one(*shards[0])
    for cut in shards[1:]:
        level = level * one(*cut)
    return level


def length_profile(count, total, most, lean):
    weights = [(1 << 20) // math.isqrt(standing ** lean) + 1 for standing in range(2, count + 1)]
    surplus, given = total - most - (count - 1), [1] * (count - 1)
    while surplus > 0:
        candidates = [i for i in range(count - 1) if given[i] < most]
        pool, budget = sum([weights[i] for i in candidates]), surplus
        for i in candidates:
            more = min(most - given[i], max(1, budget * weights[i] // pool), surplus)
            given[i] = given[i] + more
            surplus = surplus - more
    return np.array([most] + given)


def ragged(rng, amount, total, reach, slope):
    if amount == 2:
        one = jax.random.randint(rng, (), max(1, total - reach), min(reach, total - 1) + 1)
        return jnp.stack([one, total - one])
    lengths = jnp.asarray(length_profile(amount, total, reach, slope), jnp.int32)
    twos = (amount - 1) // 2
    giver, sink = lengths[1:1 + 2 * twos:2], lengths[2:2 + 2 * twos:2]
    room = jnp.minimum(giver - 1, reach - sink)
    passed = jax.random.randint(jax.random.fold_in(rng, 1), (twos,), 0, 1 << 20) % (room + 1)
    lengths = lengths.at[1:1 + 2 * twos:2].set(giver - passed).at[2:2 + 2 * twos:2].set(sink + passed)
    return lengths[jax.random.permutation(jax.random.fold_in(rng, 2), amount)]


def normal_values(rng, shape, width, bound, shards=(), kind=jnp.bfloat16):
    entries = jax.random.normal(rng, shape, jnp.float32) * width
    if len(shards) > 0:
        entries = steps_of(rng, shape, shards, -0.22, 0.18) * entries
    return jnp.clip(entries, min=-bound, max=bound).astype(kind)


def setup_inputs(seed: int = 0) -> dict:
    streams_of = jax.random.split(jax.random.key(seed), 20)
    tokens = draw_tokens(jax.random.fold_in(streams_of[19], 71), 0)
    segments = jax.vmap(lambda own: jnp.searchsorted(jnp.cumsum(ragged(own, SEGS, L, MOST, 1)), jnp.arange(L), side="right"))(jax.random.split(streams_of[1], SEQS)).reshape((SEQS, L)).astype(jnp.int32)
    cotangent = normal_values(streams_of[2], (TOKENS, D), 1.0, 6.0, ((0, 8), (1, 4)))
    in_proj = normal_values(streams_of[3], (D, 3, D), D ** -0.5, 0.1875, ((0, 4), (2, 2)), jnp.float32)
    entry_bias = normal_values(streams_of[4], (2, D), 0.05, 0.3, ((1, 2),), jnp.float32)
    out_proj = normal_values(streams_of[5], (D, D), (D * SEGS // L) ** -0.5, 2.0, ((0, 2), (1, 4)), jnp.float32)
    up_proj = normal_values(streams_of[6], (D, FF), D ** -0.5, 0.1875, ((0, 4), (1, 2)), jnp.float32)
    hidden_bias = normal_values(streams_of[7], (FF,), 0.5, 3.0, ((0, 2),), jnp.float32)
    down_proj = normal_values(streams_of[8], (FF, D), FF ** -0.5, 0.09375, ((0, 2), (1, 4)), jnp.float32)
    norm_gains = jnp.clip(1.0 + 0.1 * jax.random.normal(streams_of[9], (2, D), jnp.float32), 0.5, 1.5)
    row_biases = normal_values(streams_of[10], (4, D), 0.5, 3.0, ((1, 4),), jnp.float32)
    moments_in = draw_moments_in(jax.random.fold_in(streams_of[19], 71), 0)
    moments_entry = draw_moments_entry(jax.random.fold_in(streams_of[19], 71), 0)
    moments_out = draw_moments_out(jax.random.fold_in(streams_of[19], 71), 0)
    moments_up = draw_moments_up(jax.random.fold_in(streams_of[19], 71), 0)
    moments_hidden = draw_moments_hidden(jax.random.fold_in(streams_of[19], 71), 0)
    moments_down = draw_moments_down(jax.random.fold_in(streams_of[19], 71), 0)
    moments_gains = draw_moments_gains(jax.random.fold_in(streams_of[19], 71), 0)
    moments_biases = draw_moments_biases(jax.random.fold_in(streams_of[19], 71), 0)
    return dict(tokens=tokens, segments=segments, cotangent=cotangent, in_proj=in_proj, entry_bias=entry_bias, out_proj=out_proj, up_proj=up_proj, hidden_bias=hidden_bias, down_proj=down_proj, norm_gains=norm_gains, row_biases=row_biases, moments_in=moments_in, moments_entry=moments_entry, moments_out=moments_out, moments_up=moments_up, moments_hidden=moments_hidden, moments_down=moments_down, moments_gains=moments_gains, moments_biases=moments_biases)


LN_EPS = 1e-05
BETA_ONE = 0.9
BETA_TWO = 0.999
ADAM_EPS = 1e-08
STEP_COUNT = 2
MASK_FILL = -1e+30

def rounded(values):
    return lax.optimization_barrier(values.astype(jnp.bfloat16)).astype(jnp.float32)

def gelu_value(pre_act):
    return pre_act * (0.5 * (1.0 + lax.erf(pre_act * 2.0 ** (-0.5))))

def gelu_slope(pre_act):
    cumul = 0.5 * (1.0 + lax.erf(pre_act * 2.0 ** (-0.5)))
    density = jnp.exp(-0.5 * pre_act * pre_act) * (2.0 * jnp.pi) ** (-0.5)
    return cumul + pre_act * density

def norm_forward(inputs, gain, shift):
    mean_row = lax.optimization_barrier(jnp.mean(inputs, axis=1, keepdims=True))
    centred = inputs - mean_row
    variance = lax.optimization_barrier(jnp.mean(centred * centred, axis=1, keepdims=True))
    inv_std = lax.rsqrt(variance + LN_EPS)
    normal = centred * inv_std
    return (normal * gain + shift, normal, inv_std)

def norm_backward(upstream, normal, inv_std, gain):
    scaled = upstream * gain
    first_mean = lax.optimization_barrier(jnp.mean(scaled, axis=1, keepdims=True))
    second_mean = lax.optimization_barrier(jnp.mean(scaled * normal, axis=1, keepdims=True))
    grad = inv_std * (scaled - first_mean - normal * second_mean)
    return (grad, lax.optimization_barrier(jnp.sum(upstream * normal, axis=0)), lax.optimization_barrier(jnp.sum(upstream, axis=0)))

def seq_scores(queries, key_rows, segment):
    scaling = HD ** (-0.5)
    scores = jnp.einsum('qhd,khd->hqk', rounded(queries), rounded(key_rows)) * scaling
    same_doc = segment[:, None] == segment[None, :]
    return jnp.where(same_doc[None], scores, MASK_FILL)

def attend_forward(packed, segment):
    scores = seq_scores(packed[:, 0], packed[:, 1], segment)
    row_top = lax.optimization_barrier(jnp.max(scores, axis=-1, keepdims=True))
    log_total = row_top[..., 0] + jnp.log(lax.optimization_barrier(jnp.sum(jnp.exp(scores - row_top), axis=-1)))
    attn_probs = jnp.exp(scores - log_total[..., None])
    context = jnp.einsum('hqk,khd->qhd', rounded(attn_probs), rounded(packed[:, 2]))
    return (context.astype(jnp.bfloat16), log_total)

def attend_backward(packed, segment, log_total, grad_context):
    scaling = HD ** (-0.5)
    scores = seq_scores(packed[:, 0], packed[:, 1], segment)
    attn_probs = jnp.exp(scores - log_total[..., None])
    grad_ctx = rounded(grad_context)
    grad_values = jnp.einsum('hqk,qhd->khd', rounded(attn_probs), grad_ctx)
    grad_probs = jnp.einsum('qhd,khd->hqk', grad_ctx, rounded(packed[:, 2]))
    inner_sum = lax.optimization_barrier(jnp.sum(attn_probs * grad_probs, axis=-1, keepdims=True))
    grad_scores = rounded(attn_probs * (grad_probs - inner_sum) * scaling)
    grad_queries = jnp.einsum('hqk,khd->qhd', grad_scores, rounded(packed[:, 1]))
    grad_keys = jnp.einsum('hqk,qhd->khd', grad_scores, rounded(packed[:, 0]))
    return jnp.stack([grad_queries, grad_keys, grad_values], axis=1)

def outer_sum(left_side, right_side):
    return jnp.dot(left_side.T, right_side, preferred_element_type=jnp.float32)

def layer_block(copies, x_block, seg_block, cot_block):
    in_b, out_b, up_b, down_b, bias_three, up_bias_r, gains, biases, out_bias_r, down_bias_r = copies
    row_count = x_block.shape[0]
    mixed_qkv = jnp.dot(x_block, in_b, preferred_element_type=jnp.float32).reshape(row_count, 3, D) + bias_three
    packed = mixed_qkv.astype(jnp.bfloat16).reshape(SEQ_GRP, L, 3, HEADS, HD)
    context, log_total = lax.map(lambda member: attend_forward(member[0], member[1]), (packed, seg_block))
    context_flat = context.reshape(row_count, D)
    residual = x_block.astype(jnp.float32) + jnp.dot(context_flat, out_b, preferred_element_type=jnp.float32) + out_bias_r
    normed, normal_one, inv_one = norm_forward(residual, gains[0], biases[0])
    normed_b = normed.astype(jnp.bfloat16)
    pre_act = jnp.dot(normed_b, up_b, preferred_element_type=jnp.float32) + up_bias_r
    hidden_b = gelu_value(pre_act).astype(jnp.bfloat16)
    second = normed + jnp.dot(hidden_b, down_b, preferred_element_type=jnp.float32) + down_bias_r
    output, normal_two, inv_two = norm_forward(second, gains[1], biases[1])
    upstream = cot_block.astype(jnp.float32)
    grad_second, gain_two, shift_two = norm_backward(upstream, normal_two, inv_two, gains[1])
    grad_second_b = grad_second.astype(jnp.bfloat16)
    grad_down = outer_sum(hidden_b, grad_second_b)
    grad_pre = jnp.dot(grad_second_b, down_b.T, preferred_element_type=jnp.float32) * gelu_slope(pre_act)
    grad_pre_b = grad_pre.astype(jnp.bfloat16)
    grad_up = outer_sum(normed_b, grad_pre_b)
    grad_normed = grad_second + jnp.dot(grad_pre_b, up_b.T, preferred_element_type=jnp.float32)
    grad_resid, gain_one, shift_one = norm_backward(grad_normed, normal_one, inv_one, gains[0])
    grad_resid_b = grad_resid.astype(jnp.bfloat16)
    grad_out = outer_sum(context_flat, grad_resid_b)
    grad_context = jnp.dot(grad_resid_b, out_b.T, preferred_element_type=jnp.float32).astype(jnp.bfloat16)
    grad_context = grad_context.reshape(SEQ_GRP, L, HEADS, HD)
    grad_packed = lax.map(lambda member: attend_backward(member[0], member[1], member[2], member[3]), (packed, seg_block, log_total, grad_context))
    grad_packed = grad_packed.reshape(row_count, 3, D)
    grad_entry = jnp.stack([lax.optimization_barrier(jnp.sum(grad_packed[:, 0], axis=0)), lax.optimization_barrier(jnp.sum(grad_packed[:, 2], axis=0))])
    grad_packed_b = grad_packed.astype(jnp.bfloat16).reshape(row_count, 3 * D)
    grad_in = outer_sum(x_block, grad_packed_b).reshape(D, 3, D)
    input_grad = grad_resid + jnp.dot(grad_packed_b, in_b.T, preferred_element_type=jnp.float32)
    grads = (grad_in, grad_entry, grad_out, grad_up, lax.optimization_barrier(jnp.sum(grad_pre, axis=0)), grad_down, jnp.stack([gain_one, gain_two]), jnp.stack([shift_one, shift_two, lax.optimization_barrier(jnp.sum(grad_resid, axis=0)), lax.optimization_barrier(jnp.sum(grad_second, axis=0))]))
    return (output.astype(jnp.bfloat16), input_grad.astype(jnp.bfloat16), grads)

def adamw(grad, moments):
    first_mom = BETA_ONE * moments[0] + (1.0 - BETA_ONE) * grad
    second_mom = BETA_TWO * moments[1] + (1.0 - BETA_TWO) * grad * grad
    corr_one = 1.0 - BETA_ONE ** STEP_COUNT
    corr_two = 1.0 - BETA_TWO ** STEP_COUNT
    direction = first_mom / corr_one / (jnp.sqrt(second_mom / corr_two) + ADAM_EPS)
    return (direction, jnp.stack([first_mom, second_mom]))

def reference(tokens, segments, cotangent, in_proj, entry_bias, out_proj, up_proj, hidden_bias, down_proj, norm_gains, row_biases, moments_in, moments_entry, moments_out, moments_up, moments_hidden, moments_down, moments_gains, moments_biases):
    zero_row = jnp.zeros((D,), jnp.float32)
    bias_three = rounded(jnp.stack([entry_bias[0], zero_row, entry_bias[1]]))
    copies = (in_proj.reshape(D, 3 * D).astype(jnp.bfloat16), out_proj.astype(jnp.bfloat16), up_proj.astype(jnp.bfloat16), down_proj.astype(jnp.bfloat16), bias_three, rounded(hidden_bias), norm_gains, row_biases, rounded(row_biases[2]), rounded(row_biases[3]))
    blocks = SEQS // SEQ_GRP
    rows_block = SEQ_GRP * L
    params = (in_proj, entry_bias, out_proj, up_proj, hidden_bias, down_proj, norm_gains, row_biases)
    init = tuple((jnp.zeros(param.shape, jnp.float32) for param in params))

    def scan_step(running, member):
        output, input_grad, grads = layer_block(copies, member[0], member[1], member[2])
        return (tuple((acc + part for acc, part in zip(running, grads))), (output, input_grad))
    grads, (outputs, input_grads) = lax.scan(scan_step, init, (tokens.reshape(blocks, rows_block, D), segments.reshape(blocks, SEQ_GRP, L), cotangent.reshape(blocks, rows_block, D)))
    moments = (moments_in, moments_entry, moments_out, moments_up, moments_hidden, moments_down, moments_gains, moments_biases)
    updated = [adamw(grad, mom) for grad, mom in zip(grads, moments)]
    return (outputs.reshape(TOKENS, D), input_grads.reshape(TOKENS, D), grads[0], grads[1], grads[2], grads[3], grads[4], grads[5], grads[6], grads[7], updated[0][0], updated[1][0], updated[2][0], updated[3][0], updated[4][0], updated[5][0], updated[6][0], updated[7][0], updated[0][1], updated[1][1], updated[2][1], updated[3][1], updated[4][1], updated[5][1], updated[6][1], updated[7][1])
```

```python
import jax
import jax.numpy as jnp
from jax import lax
from jax.sharding import PartitionSpec as P

HD = 64


LN_EPS = 1e-05
BETA_ONE = 0.9
BETA_TWO = 0.999
ADAM_EPS = 1e-08
STEP_COUNT = 2
MASK_FILL = -1e30


def rounded(values):
    return lax.optimization_barrier(values.astype(jnp.bfloat16)).astype(jnp.float32)


def gelu_value(pre_act):
    return pre_act * (0.5 * (1.0 + lax.erf(pre_act * 2.0 ** (-0.5))))


def gelu_slope(pre_act):
    cumul = 0.5 * (1.0 + lax.erf(pre_act * 2.0 ** (-0.5)))
    density = jnp.exp(-0.5 * pre_act * pre_act) * (2.0 * jnp.pi) ** (-0.5)
    return cumul + pre_act * density


def spread_cols(block):
    return lax.all_gather(block, "col", axis=0, tiled=True)


def spread_rows(block):
    return lax.all_gather(block, "row", axis=0, tiled=True)


def row_totals(values):
    return lax.psum(values, "row")


def contract(left_side, right_side, flipped):
    right_dim = (1,) if flipped else (0,)
    return lax.dot_general(
        left_side, right_side, (((1,), right_dim), ((), ())), preferred_element_type=jnp.float32
    )


def outer_sum(left_side, right_side):
    return lax.dot_general(
        left_side, right_side, (((0,), (0,)), ((), ())), preferred_element_type=jnp.float32
    )


def reduce_rows(left_side, right_side, flipped):
    row_count = left_side.shape[0] // lax.axis_size("row")

    def partial_term(begin_row, length):
        return contract(left_side, right_side, flipped)

    return lax.psum_scatter(
        partial_term(jnp.int32(0), row_count * lax.axis_size("row")),
        "row",
        scatter_dimension=0,
        tiled=True,
    )


def reduce_cols(left_side, right_side, flipped):
    row_count = left_side.shape[0] // lax.axis_size("col")

    def partial_term(begin_row, length):
        return contract(left_side, right_side, flipped)

    return lax.psum_scatter(
        partial_term(jnp.int32(0), row_count * lax.axis_size("col")),
        "col",
        scatter_dimension=0,
        tiled=True,
    )


def norm_forward(inputs, gain, shift):
    full_width = inputs.shape[1] * lax.axis_size("row")
    mean_row = row_totals(jnp.sum(inputs, axis=1)) / full_width
    centred = inputs - mean_row[:, None]
    variance = row_totals(jnp.sum(centred * centred, axis=1)) / full_width
    inv_std = lax.rsqrt(variance + LN_EPS)[:, None]
    normal = centred * inv_std
    return (normal * gain + shift, normal, inv_std)


def norm_backward(upstream, normal, inv_std, gain):
    full_width = upstream.shape[1] * lax.axis_size("row")
    scaled = upstream * gain
    first_sum, second_sum = row_totals((jnp.sum(scaled, axis=1), jnp.sum(scaled * normal, axis=1)))
    grad = inv_std * (
        scaled - first_sum[:, None] / full_width - normal * (second_sum[:, None] / full_width)
    )
    return (grad, jnp.sum(upstream * normal, axis=0), jnp.sum(upstream, axis=0))


def seq_scores(queries, key_rows, segment):
    scaling = HD ** (-0.5)
    scores = (
        jnp.einsum("qhd,khd->hqk", queries, key_rows, preferred_element_type=jnp.float32) * scaling
    )
    same_doc = segment[:, None] == segment[None, :]
    return jnp.where(same_doc[None], scores, MASK_FILL)


def attend_forward(packed, segment):
    scores = seq_scores(packed[:, 0], packed[:, 1], segment)
    row_top = jnp.max(scores, axis=-1, keepdims=True)
    log_total = row_top[..., 0] + jnp.log(jnp.sum(jnp.exp(scores - row_top), axis=-1))
    attn_probs = jnp.exp(scores - log_total[..., None]).astype(jnp.bfloat16)
    context = jnp.einsum(
        "hqk,khd->qhd", attn_probs, packed[:, 2], preferred_element_type=jnp.float32
    )
    return (context.astype(jnp.bfloat16), log_total)


def attend_backward(packed, segment, log_total, grad_context):
    scaling = HD ** (-0.5)
    scores = seq_scores(packed[:, 0], packed[:, 1], segment)
    attn_probs = jnp.exp(scores - log_total[..., None])
    grad_values = jnp.einsum(
        "hqk,qhd->khd",
        attn_probs.astype(jnp.bfloat16),
        grad_context,
        preferred_element_type=jnp.float32,
    )
    grad_probs = jnp.einsum(
        "qhd,khd->hqk", grad_context, packed[:, 2], preferred_element_type=jnp.float32
    )
    inner_sum = jnp.sum(attn_probs * grad_probs, axis=-1, keepdims=True)
    grad_scores = (attn_probs * (grad_probs - inner_sum) * scaling).astype(jnp.bfloat16)
    grad_queries = jnp.einsum(
        "hqk,khd->qhd", grad_scores, packed[:, 1], preferred_element_type=jnp.float32
    )
    grad_keys = jnp.einsum(
        "hqk,qhd->khd", grad_scores, packed[:, 0], preferred_element_type=jnp.float32
    )
    return jnp.stack([grad_queries, grad_keys, grad_values], axis=1)


def adamw(grad, moments):
    first_mom = BETA_ONE * moments[0] + (1.0 - BETA_ONE) * grad
    second_mom = BETA_TWO * moments[1] + (1.0 - BETA_TWO) * grad * grad
    corr_one = 1.0 - BETA_ONE**STEP_COUNT
    corr_two = 1.0 - BETA_TWO**STEP_COUNT
    direction = first_mom / corr_one / (jnp.sqrt(second_mom / corr_two) + ADAM_EPS)
    return (direction, jnp.stack([first_mom, second_mom]))


def body(
    tokens,
    segments,
    cotangent,
    in_proj,
    entry_bias,
    out_proj,
    up_proj,
    hidden_bias,
    down_proj,
    norm_gains,
    row_biases,
    moments_in,
    moments_entry,
    moments_out,
    moments_up,
    moments_hidden,
    moments_down,
    moments_gains,
    moments_biases,
):
    width_here = tokens.shape[1]
    local_width = in_proj.shape[2]
    heads_here = local_width // HD
    seq_count = segments.shape[0]
    seq_len = segments.shape[1]
    in_b = in_proj.reshape(width_here, 3 * local_width).astype(jnp.bfloat16)
    out_b = out_proj.astype(jnp.bfloat16)
    up_b = up_proj.astype(jnp.bfloat16)
    down_b = down_proj.astype(jnp.bfloat16)
    zero_row = jnp.zeros((local_width,), jnp.float32)
    bias_three = rounded(jnp.stack([entry_bias[0], zero_row, entry_bias[1]]))
    tokens_all = spread_cols(tokens)
    mixed_flat = reduce_rows(tokens_all, in_b, False)
    mixed_qkv = mixed_flat.reshape(-1, 3, local_width) + bias_three
    packed = mixed_qkv.astype(jnp.bfloat16).reshape(seq_count, seq_len, 3, heads_here, HD)
    context, log_total = lax.map(
        lambda member: attend_forward(member[0], member[1]), (packed, segments)
    )
    context_flat = context.reshape(-1, local_width)
    context_all = spread_rows(context_flat)
    residual = (
        tokens.astype(jnp.float32) + reduce_cols(context_all, out_b, False) + rounded(row_biases[2])
    )
    normed, normal_one, inv_one = norm_forward(residual, norm_gains[0], row_biases[0])
    normed_b = normed.astype(jnp.bfloat16)
    normed_all = spread_cols(normed_b)
    pre_act = reduce_rows(normed_all, up_b, False) + rounded(hidden_bias)
    hidden_b = gelu_value(pre_act).astype(jnp.bfloat16)
    hidden_all = spread_rows(hidden_b)
    branch = reduce_cols(hidden_all, down_b, False)
    second = normed + branch + rounded(row_biases[3])
    output, normal_two, inv_two = norm_forward(second, norm_gains[1], row_biases[1])
    upstream = cotangent.astype(jnp.float32)
    grad_second, gain_two, shift_two = norm_backward(upstream, normal_two, inv_two, norm_gains[1])
    grad_second_b = grad_second.astype(jnp.bfloat16)
    grad_all = spread_cols(grad_second_b)
    grad_down = outer_sum(hidden_all, grad_all)
    grad_pre = reduce_rows(grad_all, down_b, True) * gelu_slope(pre_act)
    grad_pre_b = grad_pre.astype(jnp.bfloat16)
    grad_hidden = jnp.sum(grad_pre, axis=0)
    grad_pre_all = spread_rows(grad_pre_b)
    grad_up = outer_sum(normed_all, grad_pre_all)
    grad_from_ffn = reduce_cols(grad_pre_all, up_b, True)
    grad_normed = grad_second + grad_from_ffn
    grad_resid, gain_one, shift_one = norm_backward(grad_normed, normal_one, inv_one, norm_gains[0])
    grad_resid_b = grad_resid.astype(jnp.bfloat16)
    grad_resid_all = spread_cols(grad_resid_b)
    grad_out = outer_sum(context_all, grad_resid_all)
    grad_context = reduce_rows(grad_resid_all, out_b, True).astype(jnp.bfloat16)
    grad_context = grad_context.reshape(seq_count, seq_len, heads_here, HD)
    grad_packed = lax.map(
        lambda member: attend_backward(member[0], member[1], member[2], member[3]),
        (packed, segments, log_total, grad_context),
    )
    grad_packed = grad_packed.reshape(-1, 3, local_width)
    grad_entry = jnp.stack([jnp.sum(grad_packed[:, 0], axis=0), jnp.sum(grad_packed[:, 2], axis=0)])
    grad_packed_b = grad_packed.astype(jnp.bfloat16).reshape(-1, 3 * local_width)
    grad_packed_all = spread_rows(grad_packed_b)
    grad_in = outer_sum(tokens_all, grad_packed_all).reshape(width_here, 3, local_width)
    input_grad = (grad_resid + reduce_cols(grad_packed_all, in_b, True)).astype(jnp.bfloat16)
    grad_gains, grad_biases = lax.psum(
        (
            jnp.stack([gain_one, gain_two]),
            jnp.stack(
                [shift_one, shift_two, jnp.sum(grad_resid, axis=0), jnp.sum(grad_second, axis=0)]
            ),
        ),
        ("dp", "col"),
    )
    grad_entry, grad_hidden = lax.psum((grad_entry, grad_hidden), ("dp", "row"))
    grad_in, grad_out, grad_up, grad_down = lax.psum((grad_in, grad_out, grad_up, grad_down), "dp")
    grads = (
        grad_in,
        grad_entry,
        grad_out,
        grad_up,
        grad_hidden,
        grad_down,
        grad_gains,
        grad_biases,
    )
    moments = (
        moments_in,
        moments_entry,
        moments_out,
        moments_up,
        moments_hidden,
        moments_down,
        moments_gains,
        moments_biases,
    )
    updated = [adamw(grad, mom) for grad, mom in zip(grads, moments)]
    return (
        output.astype(jnp.bfloat16),
        input_grad,
        grads[0],
        grads[1],
        grads[2],
        grads[3],
        grads[4],
        grads[5],
        grads[6],
        grads[7],
        updated[0][0],
        updated[1][0],
        updated[2][0],
        updated[3][0],
        updated[4][0],
        updated[5][0],
        updated[6][0],
        updated[7][0],
        updated[0][1],
        updated[1][1],
        updated[2][1],
        updated[3][1],
        updated[4][1],
        updated[5][1],
        updated[6][1],
        updated[7][1],
    )


def hop_row(value, k):
    return lax.ppermute(value, "row", [(r, r ^ k) for r in range(4)])


def hop_col(value):
    return lax.ppermute(value, "col", [(0, 1), (1, 0)])


def other_core(value):
    return hop_row(value, 1)


def across_x(value):
    return hop_row(value, 2)


def gather_pieces(own, x_last):
    by_x = across_x(own)
    by_y = hop_col(own)
    both = across_x(by_y) if x_last else hop_col(by_x)
    grid = {(0, 0): own, (2, 0): by_x, (0, 1): by_y, (2, 1): both}
    for k, h in list(grid):
        grid[(k + 1, h)] = other_core(grid[(k, h)])
    return [[grid[(k, h)] for h in range(2)] for k in range(4)]


def gather_rows_small(value):
    return jnp.concatenate([value] + [hop_row(value, k) for k in (1, 2, 3)], axis=-1)


def gather_cols_small(value):
    return jnp.concatenate([value, hop_col(value)], axis=-1)


def to_sequences(tokens, length):
    me = lax.axis_index("row")
    parts = []
    for k in range(4):
        part = lax.dynamic_slice_in_dim(tokens, (me ^ k) * length, length, axis=0)
        parts.append(part if k == 0 else hop_row(part, k))
    return parts


def to_columns(blocks, length):
    me = lax.axis_index("row")
    out = jnp.zeros((4 * length, blocks[0].shape[1]), blocks[0].dtype)
    for k in range(4):
        part = blocks[k] if k == 0 else hop_row(blocks[k], k)
        out = lax.dynamic_update_slice_in_dim(out, part, (me ^ k) * length, axis=0)
    return out


def chain_sum(value):
    inward = lax.ppermute(value, "dp", [(0, 1), (3, 2)])
    half = (value.astype(jnp.float32) + inward.astype(jnp.float32)).astype(jnp.bfloat16)
    across = lax.ppermute(half, "dp", [(1, 2), (2, 1)])
    total = (half.astype(jnp.float32) + across.astype(jnp.float32)).astype(jnp.bfloat16)
    outward = lax.ppermute(total, "dp", [(1, 0), (2, 3)])
    at = lax.axis_index("dp")
    return jnp.where((at == 1) | (at == 2), total, outward).astype(jnp.float32)


def sum_pieces(make, x_first):
    def spot(first, second):
        return (2 * first, second) if x_first else (2 * second, first)

    def first_hop(value):
        return across_x(value) if x_first else hop_col(value)

    def second_hop(value):
        return hop_col(value) if x_first else across_x(value)

    def add(first, second, *others):
        k, h = spot(first, second)
        total = make(k, h)
        for other in others:
            total = total + other.astype(jnp.float32)
        return total.astype(jnp.bfloat16)

    def near(first, second):
        k, h = spot(first, second)
        return other_core(make(k + 1, h).astype(jnp.bfloat16))

    sib = {(a, b): near(a, b) for a, b in ((1, 1), (1, 0), (0, 1), (0, 0))}
    far = {b: first_hop(add(1, b, sib[(1, b)])) for b in (1, 0)}
    last = second_hop(add(0, 1, sib[(0, 1)], far[1]))
    return chain_sum(add(0, 0, sib[(0, 0)], far[0], last))


def everyone(value):
    value = value + lax.ppermute(value, "dp", [(d, d ^ 1) for d in range(4)])
    return value + lax.ppermute(value, "dp", [(d, d ^ 2) for d in range(4)])


def dot(left, right, left_dim=1, right_dim=0):
    return lax.dot_general(
        left, right, (((left_dim,), (right_dim,)), ((), ())), preferred_element_type=jnp.float32
    )


def whole_norm(inputs, gain, shift):
    mean_row = jnp.mean(inputs, axis=1, keepdims=True)
    centred = inputs - mean_row
    variance = jnp.mean(centred * centred, axis=1, keepdims=True)
    inv_std = lax.rsqrt(variance + LN_EPS)
    normal = centred * inv_std
    return (normal * gain + shift, normal, inv_std)


def whole_norm_backward(upstream, normal, inv_std, gain):
    scaled = upstream * gain
    first_mean = jnp.mean(scaled, axis=1, keepdims=True)
    second_mean = jnp.mean(scaled * normal, axis=1, keepdims=True)
    grad = inv_std * (scaled - first_mean - normal * second_mean)
    return (grad, jnp.sum(upstream * normal, axis=0), jnp.sum(upstream, axis=0))


def moving_body(
    tokens,
    segments,
    cotangent,
    in_proj,
    entry_bias,
    out_proj,
    up_proj,
    hidden_bias,
    down_proj,
    norm_gains,
    row_biases,
    moments_in,
    moments_entry,
    moments_out,
    moments_up,
    moments_hidden,
    moments_down,
    moments_gains,
    moments_biases,
):
    width = tokens.shape[1]
    half = in_proj.shape[2]
    ff_half = up_proj.shape[1]
    length = segments.shape[1]
    heads = 2 * half // HD
    row, col = lax.axis_index("row"), lax.axis_index("col")
    bf16 = jnp.bfloat16

    x_blocks = to_sequences(tokens, length)
    w_in = gather_pieces(in_proj.astype(bf16).reshape(width, 3 * half), True)
    w_out = gather_pieces(out_proj.astype(bf16), False)
    w_up = gather_pieces(up_proj.astype(bf16), True)
    w_down = gather_pieces(down_proj.astype(bf16), False)
    c_blocks = to_sequences(cotangent, length)

    seg_all = lax.all_gather(segments, "row", axis=0, tiled=True)
    segment = lax.dynamic_index_in_dim(seg_all, col * 4 + row, 0, keepdims=False)
    wide = gather_rows_small(jnp.concatenate([norm_gains, row_biases], axis=0))
    gains, biases = wide[:2], wide[2:]
    entry = gather_cols_small(entry_bias).astype(bf16).astype(jnp.float32)
    up_bias = gather_cols_small(hidden_bias).astype(bf16).astype(jnp.float32)
    out_bias = biases[2].astype(bf16).astype(jnp.float32)
    down_bias = biases[3].astype(bf16).astype(jnp.float32)

    mixed = [sum(dot(x_blocks[k], w_in[k][h]) for k in range(4)) for h in range(2)]
    mixed = jnp.concatenate([m.reshape(length, 3, half) for m in mixed], axis=2)
    bias_three = jnp.stack([entry[0], jnp.zeros_like(entry[0]), entry[1]])
    packed = (mixed + bias_three).astype(bf16).reshape(length, 3, heads, HD)
    context, log_total = attend_forward(packed, segment)
    context = context.reshape(length, 2 * half)
    c_half = [context[:, :half], context[:, half:]]
    x_all = jnp.concatenate(x_blocks, axis=1)
    branch = jnp.concatenate(
        [sum(dot(c_half[h], w_out[k][h]) for h in range(2)) for k in range(4)], axis=1
    )
    residual = x_all.astype(jnp.float32) + branch + out_bias
    normed, normal_one, inv_one = whole_norm(residual, gains[0], biases[0])
    normed_b = normed.astype(bf16)
    n_blocks = [normed_b[:, k * width : (k + 1) * width] for k in range(4)]
    pre = [
        sum(dot(n_blocks[k], w_up[k][h]) for k in range(4))
        + up_bias[h * ff_half : (h + 1) * ff_half]
        for h in range(2)
    ]
    hidden = [gelu_value(p).astype(bf16) for p in pre]
    branch = jnp.concatenate(
        [sum(dot(hidden[h], w_down[k][h]) for h in range(2)) for k in range(4)], axis=1
    )
    second = normed + branch + down_bias
    output, normal_two, inv_two = whole_norm(second, gains[1], biases[1])
    output = output.astype(bf16)
    o_blocks = [output[:, k * width : (k + 1) * width] for k in range(4)]
    layer_out = to_columns(o_blocks, length)

    upstream = jnp.concatenate(c_blocks, axis=1).astype(jnp.float32)
    grad_second, gain_two, shift_two = whole_norm_backward(upstream, normal_two, inv_two, gains[1])
    gs_b = grad_second.astype(bf16)
    gs_blocks = [gs_b[:, k * width : (k + 1) * width] for k in range(4)]
    grad_down = sum_pieces(lambda k, h: dot(hidden[h], gs_blocks[k], 0, 0), False)
    grad_pre = [
        sum(dot(gs_blocks[k], w_down[k][h], 1, 1) for k in range(4)) * gelu_slope(pre[h])
        for h in range(2)
    ]
    grad_hidden = [jnp.sum(g, axis=0) for g in grad_pre]
    gp_b = [g.astype(bf16) for g in grad_pre]
    grad_up = sum_pieces(lambda k, h: dot(n_blocks[k], gp_b[h], 0, 0), True)
    back = jnp.concatenate(
        [sum(dot(gp_b[h], w_up[k][h], 1, 1) for h in range(2)) for k in range(4)], axis=1
    )
    grad_normed = grad_second + back
    grad_resid, gain_one, shift_one = whole_norm_backward(
        grad_normed, normal_one, inv_one, gains[0]
    )
    gr_b = grad_resid.astype(bf16)
    gr_blocks = [gr_b[:, k * width : (k + 1) * width] for k in range(4)]
    grad_out = sum_pieces(lambda k, h: dot(c_half[h], gr_blocks[k], 0, 0), True)
    grad_context = jnp.concatenate(
        [sum(dot(gr_blocks[k], w_out[k][h], 1, 1) for k in range(4)) for h in range(2)], axis=1
    ).astype(bf16)
    grad_packed = attend_backward(
        packed, segment, log_total, grad_context.reshape(length, heads, HD)
    ).reshape(length, 3, 2 * half)
    grad_entry = jnp.stack([jnp.sum(grad_packed[:, 0], axis=0), jnp.sum(grad_packed[:, 2], axis=0)])
    gk_b = grad_packed.astype(bf16)
    gk_half = [gk_b[:, :, h * half : (h + 1) * half].reshape(length, 3 * half) for h in range(2)]
    grad_in = sum_pieces(lambda k, h: dot(x_blocks[k], gk_half[h], 0, 0), False)
    back = [sum(dot(gk_half[h], w_in[k][h], 1, 1) for h in range(2)) for k in range(4)]
    i_blocks = [
        (grad_resid[:, k * width : (k + 1) * width] + back[k]).astype(bf16) for k in range(4)
    ]
    input_grad = to_columns(i_blocks, length)

    tall = jnp.stack(
        [
            gain_one,
            gain_two,
            shift_one,
            shift_two,
            jnp.sum(grad_resid, axis=0),
            jnp.sum(grad_second, axis=0),
        ]
    )
    mine = tall[:, :width]
    for k in (1, 2, 3):
        mine = mine + hop_row(tall[:, k * width : (k + 1) * width], k)
    mine = mine + hop_col(mine)
    own_half = jnp.concatenate([grad_entry[:, :half].reshape(-1), grad_hidden[0]])
    far_half = jnp.concatenate([grad_entry[:, half:].reshape(-1), grad_hidden[1]])
    both = own_half + hop_col(far_half)
    both = both + other_core(both)
    both = both + across_x(both)
    flat = everyone(jnp.concatenate([mine.reshape(-1), both]))
    mine, both = flat[: 6 * width].reshape(6, width), flat[6 * width :]
    grad_gains, grad_biases = mine[:2], mine[2:]
    grad_entry, grad_hidden = both[: 2 * half].reshape(2, half), both[2 * half :]

    grads = (
        grad_in.reshape(width, 3, half),
        grad_entry,
        grad_out,
        grad_up,
        grad_hidden,
        grad_down,
        grad_gains,
        grad_biases,
    )
    moments = (
        moments_in,
        moments_entry,
        moments_out,
        moments_up,
        moments_hidden,
        moments_down,
        moments_gains,
        moments_biases,
    )
    updated = [adamw(grad, mom) for grad, mom in zip(grads, moments)]
    return (
        (layer_out, input_grad)
        + grads
        + tuple(u[0] for u in updated)
        + tuple(u[1] for u in updated)
    )


def solution(mesh):
    in_specs = (
        P(("dp", "col"), "row"),
        P(("dp", "row"), None),
        P(("dp", "col"), "row"),
        P("row", None, "col"),
        P(None, "col"),
        P("col", "row"),
        P("row", "col"),
        P("col"),
        P("col", "row"),
        P(None, "row"),
        P(None, "row"),
        P(None, "row", None, "col"),
        P(None, None, "col"),
        P(None, "col", "row"),
        P(None, "row", "col"),
        P(None, "col"),
        P(None, "col", "row"),
        P(None, None, "row"),
        P(None, None, "row"),
    )
    out_specs = (
        P(("dp", "col"), "row"),
        P(("dp", "col"), "row"),
        P("row", None, "col"),
        P(None, "col"),
        P("col", "row"),
        P("row", "col"),
        P("col"),
        P("col", "row"),
        P(None, "row"),
        P(None, "row"),
        P("row", None, "col"),
        P(None, "col"),
        P("col", "row"),
        P("row", "col"),
        P("col"),
        P("col", "row"),
        P(None, "row"),
        P(None, "row"),
        P(None, "row", None, "col"),
        P(None, None, "col"),
        P(None, "col", "row"),
        P(None, "row", "col"),
        P(None, "col"),
        P(None, "col", "row"),
        P(None, None, "row"),
        P(None, None, "row"),
    )

    def step(*args):
        sizes = dict(mesh.shape)
        sequences = args[1].shape[0] // (sizes["dp"] * sizes["col"])
        fits = sizes == {"dp": 4, "row": 4, "col": 2} and sequences == sizes["row"]
        chosen = moving_body if fits else body
        return jax.shard_map(
            chosen, mesh=mesh, in_specs=in_specs, out_specs=out_specs, check_vma=False
        )(*args)

    return step
```
